32 devices in a mesh: seq: 16 (over z, y, core), head: 2 (over x).
Axes of the slice: x: 2, y: 2, z: 4, core: 2. Of those that a mesh axis runs over, the one named last changes fastest.
Arguments:
- queries: bfloat16 [4, 64, 64, 128], P(None, None, 'head'), may hold values from -15 to 15
- new_keys: bfloat16 [4, 64, 8, 128], P(None, None, 'head'), may hold values from -16 to 16
- new_values: bfloat16 [4, 64, 8, 128], P(None, None, 'head'), may hold values from -6 to 6
- cache_keys: bfloat16 [4, 32768, 8, 128], P(None, 'seq', 'head'), may hold values from -6 to 6
- cache_values: bfloat16 [4, 32768, 8, 128], P(None, 'seq', 'head'), may hold values from -6 to 6
- parents: int32 [4, 64], replicated, may hold values from 0 to 63, as said below
- kv_lengths: int32 [4], replicated, may hold values from 1 to 32768
- out_weight: bfloat16 [8192, 8192], P('head', 'seq'), may hold values from -0.5 to 0.5
Outputs:
- mixed: bfloat16 [256, 8192], P('head', 'seq')
The draws below stay inside these ranges and needn't reach their ends.
Inputs may be any that keep to these rules, and one draw needn't show every extreme that they name: parents[r, 0] = 0 for the root; for i >= 1, parents[r, i] < i.
All inputs are finite; a program needn't handle non-finite values.
Results may differ from the reference program's by a relative error of at most 0.0045.
Values may be sent and summed in bfloat16 or wider, within the bound.
A program may use at most 128 MiB of HBM per device.

```python
import jax
import jax.numpy as jnp
from jax import lax

D = 8192
H = 64
KVH = 8
HD = 128
TREE = 64
REQS = 4
L = 32768
N_SEQ = 16


def drawn_pair(key):
    base_key = jax.random.fold_in(key, 11)
    key_query, key_draft = jax.random.split(base_key, 2)
    queries = jnp.clip(2.5 * jax.random.normal(key_query, (REQS, TREE, H, HD), jnp.float32), -15.0, 15.0)
    drafts = jnp.clip(4.0 * jax.random.normal(key_draft, (REQS, TREE, KVH, HD), jnp.float32), -16.0, 16.0)
    return (queries, drafts)


def draw_queries(key, part):
    return drawn_pair(key)[0].astype(jnp.bfloat16)


def draw_new_keys(key, part):
    return drawn_pair(key)[1].astype(jnp.bfloat16)


def draw_parents(key, part):
    tree_key = jax.random.fold_in(key, 5)
    indices = jnp.arange(TREE, dtype=jnp.int32)
    upper = jnp.maximum(indices, 1)
    raw_parents = jax.random.randint(tree_key, (REQS, TREE), 0, upper[None, :])
    return (raw_parents * (indices > 0)[None, :]).astype(jnp.int32)


def set_ends(result, rng, least, largest):
    place = [jax.random.randint(jax.random.fold_in(rng, axis), (), 0, length) for axis, length in enumerate(result.shape)]
    longest = result.shape.index(max(result.shape))
    neighbour = place[:longest] + [(place[longest] + 1) % result.shape[longest]] + place[longest + 1:]
    return result.at[tuple(place)].set(least).at[tuple(neighbour)].set(largest)


def level_of(own_key, dims, cuts, smallest, high):
    def one(dim, parts):
        heights = jax.random.uniform(jax.random.fold_in(jax.random.fold_in(own_key, 6), dim), (parts,), jnp.float32, smallest / len(cuts), high / len(cuts))
        return jnp.repeat(jnp.exp(heights), dims[dim] // parts).reshape((-1,) + (1,) * (len(dims) - dim - 1))

    gain = one(*cuts[0])
    for cut in cuts[1:]:
        gain = gain * one(*cut)
    return gain


def bell_draw(own_key, dims, width, bound, cuts=(), kind=jnp.bfloat16):
    drawn = jax.random.normal(own_key, dims, jnp.float32) * width
    if len(cuts) > 0:
        drawn = level_of(own_key, dims, cuts, -0.22, 0.18) * drawn
    return jnp.clip(drawn, min=-bound, max=bound).astype(kind)


def setup_inputs(seed: int = 0) -> dict:
    arg_keys = jax.random.split(jax.random.key(seed), 9)
    queries = draw_queries(jax.random.fold_in(arg_keys[8], 71), 0)
    new_keys = draw_new_keys(jax.random.fold_in(arg_keys[8], 71), 0)
    new_values = bell_draw(arg_keys[2], (REQS, TREE, KVH, HD), 1.0, 6.0, ((2, 2),))
    cache_keys = bell_draw(arg_keys[3], (REQS, L, KVH, HD), 1.0, 6.0, ((1, 16), (2, 2)))
    cache_values = bell_draw(arg_keys[4], (REQS, L, KVH, HD), 1.0, 6.0, ((1, 16), (2, 2)))
    parents = draw_parents(jax.random.fold_in(arg_keys[8], 71), 0)
    kv_lengths = set_ends(jax.random.randint(arg_keys[6], (REQS,), 1, L + 1), jax.random.fold_in(arg_keys[6], 1), 1, L).astype(jnp.int32)
    out_weight = bell_draw(arg_keys[7], (H * HD, D), HD ** -0.5, 0.5, ((0, 2), (1, 16)))
    return dict(queries=queries, new_keys=new_keys, new_values=new_values, cache_keys=cache_keys, cache_values=cache_values, parents=parents, kv_lengths=kv_lengths, out_weight=out_weight)


lowest = -1.0e30


def ancestors(parent_row):
    tree_size = parent_row.shape[0]
    indices = jnp.arange(tree_size, dtype=jnp.int32)
    parent_link = (parent_row[:, None] == indices[None, :]).astype(jnp.float32)
    itself = (indices[:, None] == indices[None, :]).astype(jnp.float32)
    reached = jnp.maximum(parent_link, itself)
    for repeat in range(max(1, (tree_size - 1).bit_length())):
        reached = jnp.minimum(jnp.dot(reached, reached, precision=lax.Precision.HIGHEST), 1.0)
    return reached


def block_partial(query_rows, keys, values, allowed, score_scale):
    scores = jnp.dot(query_rows, keys.T, preferred_element_type=jnp.float32) * score_scale
    scores = jnp.where(allowed, scores, lowest)
    maxima = jnp.max(scores, axis=-1)
    weights = jnp.where(allowed, jnp.exp(scores - maxima[:, None]), 0.0)
    totals = jnp.sum(weights, axis=-1)
    weighted = jnp.dot(weights.astype(jnp.bfloat16), values, preferred_element_type=jnp.float32)
    return maxima, totals, weighted


def reference(queries, new_keys, new_values, cache_keys, cache_values, parents, kv_lengths, out_weight):
    requests, tree_size, heads, head_size = queries.shape
    kv_heads = new_keys.shape[2]
    group_size = heads // kv_heads
    cache_len = cache_keys.shape[1]
    block_size = cache_len // N_SEQ
    score_scale = 1.0 / (head_size ** 0.5)
    positions = jnp.arange(cache_len, dtype=jnp.int32).reshape(N_SEQ, block_size)

    def one_request(request_items):
        query, tree_keys, tree_values, past_keys, past_values, parent_row, length = request_items
        query_rows = query.reshape(tree_size, kv_heads, group_size, head_size).transpose(1, 0, 2, 3)
        query_rows = query_rows.reshape(kv_heads, tree_size * group_size, head_size)
        tree_allowed = jnp.repeat(ancestors(parent_row), group_size, axis=0) > 0.5
        cache_allowed = positions < length

        def one_head(head_items):
            head_rows, head_tree_keys, head_tree_values, head_past_keys, head_past_values = head_items
            blocked_keys = head_past_keys.reshape(N_SEQ, block_size, head_size)
            blocked_values = head_past_values.reshape(N_SEQ, block_size, head_size)
            cache_max, cache_tot, cache_acc = jax.vmap(block_partial, in_axes=(None, 0, 0, 0, None))(
                head_rows, blocked_keys, blocked_values, cache_allowed, score_scale)
            tree_max, tree_tot, tree_acc = block_partial(head_rows, head_tree_keys, head_tree_values, tree_allowed, score_scale)
            maxima = jnp.concatenate([cache_max, tree_max[None]], axis=0)
            totals = jnp.concatenate([cache_tot, tree_tot[None]], axis=0)
            weighted = jnp.concatenate([cache_acc, tree_acc[None]], axis=0)
            overall = jnp.max(maxima, axis=0)
            factor = jnp.exp(maxima - overall[None])
            total = jnp.sum(totals * factor, axis=0)
            merged = jnp.sum(weighted * factor[:, :, None], axis=0)
            return (merged / total[:, None]).astype(jnp.bfloat16)

        attended = lax.map(one_head, (query_rows, tree_keys.transpose(1, 0, 2), tree_values.transpose(1, 0, 2),
                                      past_keys.transpose(1, 0, 2), past_values.transpose(1, 0, 2)))
        attended = attended.reshape(kv_heads, tree_size, group_size, head_size).transpose(1, 0, 2, 3)
        return attended.reshape(tree_size, heads * head_size)

    attended = lax.map(one_request, (queries, new_keys, new_values, cache_keys, cache_values, parents, kv_lengths))
    attended = attended.reshape(requests * tree_size, heads * head_size)
    return jnp.dot(attended, out_weight, preferred_element_type=jnp.float32).astype(jnp.bfloat16)
```

```python
import functools
import math

import jax
import jax.numpy as jnp
from jax import lax
from jax.experimental import pallas as pl
from jax.experimental.pallas import tpu as pltpu
from jax.sharding import PartitionSpec as P

lowest = -1e30
NT = (((1,), (1,)), ((), ()))
TN = (((0,), (0,)), ((), ()))


def bit_reversed(index, stages):
    result = index * 0
    for stage in range(stages):
        result = result * 2 + (index // (1 << stage)) % 2
    return result


def attend_kernel(kv_heads, split, stages, score_scale, lengths_ref, place_ref, q_ref, k_ref, v_ref,
                  tk_ref, tv_ref, parents_ref, o_ref, ml_ref):
    step = pl.program_id(0)
    block_size = k_ref.shape[0]
    columns = q_ref.shape[0]
    tile = min(256, columns)
    request = step // kv_heads
    me = place_ref[0]
    valid = lengths_ref[request] - me * block_size

    def write(masked):
        for start in range(0, columns, tile):
            here = pl.ds(start, tile)
            s = lax.dot_general(k_ref[...], q_ref[here, :], NT, preferred_element_type=jnp.float32)
            if masked:
                rows = lax.broadcasted_iota(jnp.int32, s.shape, 0)
                s = jnp.where(rows < valid, s, lowest)
            m = jnp.max(s, axis=0, keepdims=True) * score_scale
            w = jnp.exp2(s * score_scale - m)
            ml_ref[0, here] = m[0]
            ml_ref[1, here] = jnp.sum(w, axis=0)
            o_ref[:, here] = lax.dot_general(
                v_ref[...], w.astype(jnp.bfloat16), TN, preferred_element_type=jnp.float32
            ).astype(o_ref.dtype)

    @pl.when(valid >= block_size)
    def _():
        write(False)

    @pl.when((valid > 0) & (valid < block_size))
    def _():
        write(True)

    @pl.when(valid <= 0)
    def _():
        o_ref[...] = jnp.zeros_like(o_ref)
        ml_ref[0, :] = jnp.full((columns,), lowest, jnp.float32)
        ml_ref[1, :] = jnp.zeros((columns,), jnp.float32)

    own = bit_reversed(me, stages)

    @pl.when((own // split == step) & (own % split == 0))
    def _():
        tree = tk_ref.shape[0]

        def reach(parent_row):
            width = parent_row.shape[1]
            key = lax.broadcasted_iota(jnp.int32, (tree, width), 0)
            token = lax.broadcasted_iota(jnp.int32, (tree, width), 1) % tree
            hit = (parent_row == key) | (token == key)
            return jnp.where(hit, 1.0, 0.0)

        wide = reach(parents_ref[0:1, :])
        square = wide[:, :tree]
        for _ in range(max(1, (tree - 1).bit_length())):
            left = square.astype(jnp.bfloat16)
            wide = jnp.minimum(jnp.dot(left, wide.astype(jnp.bfloat16), preferred_element_type=jnp.float32), 1.0)
            square = wide[:, :tree]
        s = lax.dot_general(tk_ref[...], q_ref[...], NT, preferred_element_type=jnp.float32)
        allowed = wide > 0.5
        s = jnp.where(allowed, s * score_scale, lowest)
        m = jnp.max(s, axis=0, keepdims=True)
        w = jnp.where(allowed, jnp.exp2(s - m), 0.0)
        tot = jnp.sum(w, axis=0, keepdims=True)
        acc = lax.dot_general(tv_ref[...], w.astype(jnp.bfloat16), TN, preferred_element_type=jnp.float32)
        m_old = ml_ref[0:1, :]
        m_new = jnp.maximum(m_old, m)
        f_old, f_tree = jnp.exp2(m_old - m_new), jnp.exp2(m - m_new)
        ml_ref[1:2, :] = ml_ref[1:2, :] * f_old + tot * f_tree
        ml_ref[0:1, :] = m_new
        o_ref[...] = (o_ref[...].astype(jnp.float32) * f_old + acc * f_tree).astype(o_ref.dtype)


def merge_kernel(n, stages, split, turn, o_ref, ml_ref, g_ref, *scratch):
    per = 4
    o_cur = [o_ref] + list(scratch[0:stages])
    ml_cur = [ml_ref] + list(scratch[stages:2 * stages])
    o_in = scratch[2 * stages:3 * stages]
    ml_in = scratch[3 * stages:4 * stages]
    send, recv = scratch[4 * stages], scratch[4 * stages + 1]
    me = lax.axis_index("seq")
    bits = [(me // (1 << s)) % 2 for s in range(stages)]
    partners = [me + (1 - 2 * bits[s]) * (1 << s) for s in range(stages)]

    barrier = pltpu.get_barrier_semaphore()
    for s in range(stages):
        pl.semaphore_signal(barrier, inc=1, device_id={"seq": partners[s]}, device_id_type=pl.DeviceIdType.MESH)
    pl.semaphore_wait(barrier, stages)

    def remote(src, dst, slot, s):
        return pltpu.make_async_remote_copy(
            src_ref=src, dst_ref=dst, send_sem=send.at[slot], recv_sem=recv.at[slot],
            device_id={"seq": partners[s]}, device_id_type=pl.DeviceIdType.MESH,
        )

    waits = []
    for s in range(stages):
        half = n >> (s + 1)
        pairs = max(1, half // split)
        away, keep = (1 - bits[s]) * half, bits[s] * half
        pair_away, pair_keep = ((1 - bits[s]) * pairs, bits[s] * pairs) if half >= split else (0, 0)
        first = remote(o_cur[s].at[pl.ds(away, half)], o_in[s], 2 * s, s)
        second = remote(ml_cur[s].at[pl.ds(pair_away, pairs)], ml_in[s], 2 * s + 1, s)
        second.start()
        first.start()
        waits += [first, second]
        second.wait_recv()
        first.wait_recv()
        per_pair = half // pairs

        def one_pair(p, carry, s=s, keep=keep, pair_keep=pair_keep, per_pair=per_pair):
            m_a, m_b = ml_cur[s][pair_keep + p, 0:1, :], ml_in[s][p, 0:1, :]
            l_a, l_b = ml_cur[s][pair_keep + p, 1:2, :], ml_in[s][p, 1:2, :]
            m = jnp.maximum(m_a, m_b)
            f_a, f_b = jnp.exp2(m_a - m), jnp.exp2(m_b - m)
            ml_cur[s + 1][p, 0:1, :] = m
            ml_cur[s + 1][p, 1:2, :] = l_a * f_a + l_b * f_b
            for c in range(per_pair):
                at = p * per_pair + c
                mine = o_cur[s][keep + at].astype(jnp.float32)
                theirs = o_in[s][at].astype(jnp.float32)
                o_cur[s + 1][at] = (mine * f_a + theirs * f_b).astype(o_cur[s + 1].dtype)
            return carry

        lax.fori_loop(0, pairs, one_pair, 0)

    low = bit_reversed(me, stages)
    share = o_cur[stages][0].astype(jnp.float32) / ml_cur[stages][0, 1:2, :]
    if turn:
        share = share.T
    g_ref[low] = share.astype(g_ref.dtype)
    for s in reversed(range(stages)):
        size = n >> (s + 1)
        start = (low // size) * size
        block = g_ref.at[pl.ds(start, size)]
        copy = remote(block, block, 2 * stages + s, s)
        copy.start()
        waits.append(copy)
        copy.wait_recv()
    for copy in waits:
        copy.wait_send()


def body(queries, new_keys, new_values, cache_keys, cache_values, parents, kv_lengths, out_weight):
    requests, tree, heads, head_size = queries.shape
    kv_heads = new_keys.shape[2]
    group = heads // kv_heads
    block_size = cache_keys.shape[1]
    n = lax.axis_size("seq")
    stages = n.bit_length() - 1
    pairs = requests * kv_heads
    split = max(1, n // pairs)
    columns = group * tree
    deep = head_size * pairs // n
    me = lax.axis_index("seq")
    score_scale = math.log2(math.e) / math.sqrt(head_size)

    def by_head(array):
        return array.transpose(0, 2, 1, 3).reshape(pairs, array.shape[1], head_size)

    q = queries.reshape(requests, tree, kv_heads, group, head_size).transpose(0, 2, 3, 1, 4)
    q = q.reshape(pairs, columns, head_size)
    parent_rows = jnp.broadcast_to(jnp.tile(parents, (1, group))[:, None, :], (requests, 8, columns))

    def pair_block(rows):
        return pl.BlockSpec((None, rows, head_size), lambda p, *_: (p, 0, 0))

    o, ml = pl.pallas_call(
        functools.partial(attend_kernel, kv_heads, split, stages, score_scale),
        grid_spec=pltpu.PrefetchScalarGridSpec(
            num_scalar_prefetch=2,
            grid=(pairs,),
            in_specs=[
                pair_block(columns), pair_block(block_size), pair_block(block_size),
                pair_block(tree), pair_block(tree),
                pl.BlockSpec((None, 8, columns), lambda p, *_: (p // kv_heads, 0, 0)),
            ],
            out_specs=[
                pl.BlockSpec((None, head_size, columns), lambda p, *_: (p, 0, 0)),
                pl.BlockSpec((None, 2, columns), lambda p, *_: (p, 0, 0)),
            ],
        ),
        out_shape=[
            jax.ShapeDtypeStruct((pairs, head_size, columns), jnp.bfloat16),
            jax.ShapeDtypeStruct((pairs, 2, columns), jnp.float32),
        ],
        compiler_params=pltpu.CompilerParams(vmem_limit_bytes=48 * 1024 * 1024),
    )(kv_lengths, me[None].astype(jnp.int32), q, by_head(cache_keys), by_head(cache_values),
      by_head(new_keys), by_head(new_values), parent_rows)

    turn = split == 1 and deep == head_size
    o = o.reshape(n, deep, columns)
    piece = (columns, deep) if turn else (deep, columns)
    halves = [n >> (s + 1) for s in range(stages)]
    o_bufs = [pltpu.VMEM((h, deep, columns), jnp.bfloat16) for h in halves]
    ml_bufs = [pltpu.VMEM((max(1, h // split), 2, columns), jnp.float32) for h in halves]
    vmem = pl.BlockSpec(memory_space=pltpu.VMEM)
    gathered = pl.pallas_call(
        functools.partial(merge_kernel, n, stages, split, turn),
        out_shape=jax.ShapeDtypeStruct((n,) + piece, jnp.bfloat16),
        in_specs=[vmem, vmem],
        out_specs=vmem,
        scratch_shapes=o_bufs + ml_bufs + o_bufs + ml_bufs
        + [pltpu.SemaphoreType.DMA((3 * stages,)), pltpu.SemaphoreType.DMA((3 * stages,))],
        compiler_params=pltpu.CompilerParams(
            collective_id=0, has_side_effects=True, vmem_limit_bytes=32 * 1024 * 1024
        ),
    )(o, ml)
    if turn:
        attended = gathered.reshape(requests, kv_heads, group, tree, head_size).transpose(0, 3, 1, 2, 4)
    else:
        attended = gathered.reshape(requests, kv_heads, head_size, group, tree).transpose(0, 4, 1, 3, 2)
    attended = attended.reshape(requests * tree, heads * head_size)
    mixed = lax.psum_scatter(
        jnp.dot(attended, out_weight, preferred_element_type=jnp.float32),
        "head",
        scatter_dimension=0,
        tiled=True,
    )
    return mixed.astype(jnp.bfloat16)


def solution(mesh):
    placed = (
        P(None, None, "head", None),
        P(None, None, "head", None),
        P(None, None, "head", None),
        P(None, "seq", "head", None),
        P(None, "seq", "head", None),
        P(),
        P(),
        P("head", "seq"),
    )
    return jax.shard_map(
        body, mesh=mesh, in_specs=placed, out_specs=P("head", "seq"), check_vma=False
    )
```

```python
import functools
import math

import jax
import jax.numpy as jnp
from jax import lax
from jax.experimental import pallas as pl
from jax.experimental.pallas import tpu as pltpu
from jax.sharding import PartitionSpec as P

lowest = -1e30
NT = (((1,), (1,)), ((), ()))
TN = (((0,), (0,)), ((), ()))


def bit_reversed(index, stages):
    result = index * 0
    for stage in range(stages):
        result = result * 2 + (index // (1 << stage)) % 2
    return result


def attend_kernel(kv_heads, split, stages, score_scale, lengths_ref, place_ref, q_ref, k_ref, v_ref,
                  tk_ref, tv_ref, parents_ref, o_ref, ml_ref):
    step = pl.program_id(0)
    block_size = k_ref.shape[0]
    columns = q_ref.shape[0]
    tile = min(256, columns)
    streams, _, lanes = o_ref.shape
    request = step // kv_heads
    me = place_ref[0]
    valid = lengths_ref[request] - me * block_size

    def write(masked):
        for start in range(0, columns, tile):
            here = pl.ds(start, tile)
            s = lax.dot_general(k_ref[...], q_ref[here, :], NT, preferred_element_type=jnp.float32)
            if masked:
                rows = lax.broadcasted_iota(jnp.int32, s.shape, 0)
                s = jnp.where(rows < valid, s, lowest)
            m = jnp.max(s, axis=0, keepdims=True) * score_scale
            w = jnp.exp2(s * score_scale - m)
            tot = jnp.sum(w, axis=0, keepdims=True)
            acc = lax.dot_general(
                v_ref[...], w.astype(jnp.bfloat16), TN, preferred_element_type=jnp.float32
            ).astype(o_ref.dtype)
            for inner in range(0, tile, lanes):
                t = (start + inner) // lanes
                ml_ref[t, 0:1, :] = m[:, inner:inner + lanes]
                ml_ref[t, 1:2, :] = tot[:, inner:inner + lanes]
                o_ref[t] = acc[:, inner:inner + lanes]

    @pl.when(valid >= block_size)
    def _():
        write(False)

    @pl.when((valid > 0) & (valid < block_size))
    def _():
        write(True)

    @pl.when(valid <= 0)
    def _():
        o_ref[...] = jnp.zeros_like(o_ref)
        ml_ref[:, 0:1, :] = jnp.full((streams, 1, lanes), lowest, jnp.float32)
        ml_ref[:, 1:2, :] = jnp.zeros((streams, 1, lanes), jnp.float32)

    own = bit_reversed(me, stages)

    @pl.when((own // split == step) & (own % split == 0))
    def _():
        tree = tk_ref.shape[0]

        def reach(parent_row):
            width = parent_row.shape[1]
            key = lax.broadcasted_iota(jnp.int32, (tree, width), 0)
            token = lax.broadcasted_iota(jnp.int32, (tree, width), 1) % tree
            hit = (parent_row == key) | (token == key)
            return jnp.where(hit, 1.0, 0.0)

        wide = reach(parents_ref[0:1, :])
        square = wide[:, :tree]
        for _ in range(max(1, (tree - 1).bit_length())):
            left = square.astype(jnp.bfloat16)
            wide = jnp.minimum(jnp.dot(left, wide.astype(jnp.bfloat16), preferred_element_type=jnp.float32), 1.0)
            square = wide[:, :tree]
        s = lax.dot_general(tk_ref[...], q_ref[...], NT, preferred_element_type=jnp.float32)
        allowed = wide > 0.5
        s = jnp.where(allowed, s * score_scale, lowest)
        m = jnp.max(s, axis=0, keepdims=True)
        w = jnp.where(allowed, jnp.exp2(s - m), 0.0)
        tot = jnp.sum(w, axis=0, keepdims=True)
        acc = lax.dot_general(tv_ref[...], w.astype(jnp.bfloat16), TN, preferred_element_type=jnp.float32)
        for t in range(streams):
            here = slice(t * lanes, (t + 1) * lanes)
            m_old = ml_ref[t, 0:1, :]
            m_new = jnp.maximum(m_old, m[:, here])
            f_old, f_tree = jnp.exp2(m_old - m_new), jnp.exp2(m[:, here] - m_new)
            ml_ref[t, 1:2, :] = ml_ref[t, 1:2, :] * f_old + tot[:, here] * f_tree
            ml_ref[t, 0:1, :] = m_new
            o_ref[t] = (o_ref[t].astype(jnp.float32) * f_old + acc[:, here] * f_tree).astype(o_ref.dtype)


def merge_kernel(n, stages, split, orders, masks, head_axis, fused, o_ref, ml_ref, *refs):
    streams = len(orders)
    if fused:
        w_ref, out_ref, *scratch = refs
    else:
        g_ref, *scratch = refs
    scratch = list(scratch)

    def take(count):
        taken = scratch[:count]
        del scratch[:count]
        return taken

    o_sum, o_out, o_in, ml_out, ml_in = (take(stages) for _ in range(5))
    (send, recv) = take(2)
    me = lax.axis_index("seq")

    def bit(position):
        return (me // (1 << position)) % 2

    partners, bits = [], []
    for position in range(stages):
        move = 0
        for q in range(stages):
            if (masks[position] >> q) & 1:
                move = move + (1 - 2 * bit(q)) * (1 << q)
        partners.append(me + move)
        value = bit(position)
        for other in range(position + 1, stages):
            if (masks[other] >> position) & 1:
                value = (value + bit(other)) % 2
        bits.append(value)

    head_stages = []
    if fused:
        (attended, product) = take(2)
        head_count = lax.axis_size(head_axis)
        head_stages = take(head_count.bit_length() - 1)
        (head_send, head_recv) = take(2)
        head = lax.axis_index(head_axis)

    barrier = pltpu.get_barrier_semaphore()
    for partner in partners:
        pl.semaphore_signal(barrier, inc=1, device_id={"seq": partner}, device_id_type=pl.DeviceIdType.MESH)
    head_plan = []
    for s in range(len(head_stages)):
        stride = head_count >> (s + 1)
        head_bit = (head // stride) % 2
        partner = head + (1 - 2 * head_bit) * stride
        head_plan.append((head_bit, partner))
        pl.semaphore_signal(barrier, inc=1, device_id={head_axis: partner}, device_id_type=pl.DeviceIdType.MESH)
    pl.semaphore_wait(barrier, stages + len(head_stages))

    def remote(src, dst, slot, position):
        return pltpu.make_async_remote_copy(
            src_ref=src, dst_ref=dst, send_sem=send.at[slot], recv_sem=recv.at[slot],
            device_id={"seq": partners[position]}, device_id_type=pl.DeviceIdType.MESH,
        )

    waits = []
    flying = {}

    def begin(t, s):
        position = orders[t][s]
        half = n >> (s + 1)
        pairs = max(1, half // split)
        away = (1 - bits[position]) * half
        pair_away = (1 - bits[position]) * pairs if half >= split else 0
        o_src = o_ref if s == 0 else o_out[s - 1]
        ml_src = ml_ref if s == 0 else ml_out[s - 1]
        slot = (t * stages + s) * 3
        small = remote(ml_src.at[t, pl.ds(pair_away, pairs)], ml_in[s].at[t], slot, position)
        large = remote(o_src.at[t, pl.ds(away, half)], o_in[s].at[t], slot + 1, position)
        small.start()
        large.start()
        waits.extend([small, large])
        flying[t] = (small, large)

    def finish(t, s):
        position = orders[t][s]
        half = n >> (s + 1)
        pairs = max(1, half // split)
        keep = bits[position] * half
        pair_keep = bits[position] * pairs if half >= split else 0
        per_pair = half // pairs
        small, large = flying[t]
        small.wait_recv()
        large.wait_recv()
        ml_src = ml_ref if s == 0 else ml_out[s - 1]
        o_src = o_ref if s == 0 else o_sum[s - 1]

        def one_pair(p, carry):
            m_a, m_b = ml_src[t, pair_keep + p, 0:1, :], ml_in[s][t, p, 0:1, :]
            l_a, l_b = ml_src[t, pair_keep + p, 1:2, :], ml_in[s][t, p, 1:2, :]
            m = jnp.maximum(m_a, m_b)
            f_a, f_b = jnp.exp2(m_a - m), jnp.exp2(m_b - m)
            ml_out[s][t, p, 0:1, :] = m
            ml_out[s][t, p, 1:2, :] = l_a * f_a + l_b * f_b
            for c in range(per_pair):
                at = p * per_pair + c
                mine = o_src[t, keep + at].astype(jnp.float32)
                theirs = o_in[s][t, at].astype(jnp.float32)
                total = mine * f_a + theirs * f_b
                o_sum[s][t, at] = total
                o_out[s][t, at] = total.astype(jnp.bfloat16)
            return carry

        lax.fori_loop(0, pairs, one_pair, 0)

    for t in range(streams):
        begin(t, 0)
    lows = [0] * streams
    gathered = attended if fused else g_ref

    def gather(t, s):
        size = n >> (s + 1)
        start = (lows[t] // size) * size
        block = gathered.at[t, pl.ds(start, size)]
        copy = remote(block, block, (t * stages + s) * 3 + 2, orders[t][s])
        copy.start()
        waits.append(copy)
        flying[t] = copy

    for s in range(stages):
        for t in range(streams):
            finish(t, s)
            if s + 1 < stages:
                begin(t, s + 1)
            else:
                low = 0
                for position in orders[t]:
                    low = low * 2 + bits[position]
                lows[t] = low
                share = o_sum[s][t, 0] / ml_out[s][t, 0, 1:2, :]
                if fused:
                    share = share.T
                gathered[t, low] = share.astype(jnp.bfloat16)
                gather(t, s)
    for s in reversed(range(stages)):
        for t in range(streams):
            flying[t].wait_recv()
            if s > 0:
                gather(t, s - 1)

    if fused:
        tokens, width = product.shape
        requests, tree = fused
        kv_heads = n // requests
        parts = attended.shape[2] // tree
        groups = streams * parts
        head_size = attended.shape[3]

        def rows_of(request):
            pieces = []
            for k in range(kv_heads):
                for t in range(streams):
                    for g in range(parts):
                        pieces.append(attended[t, request * kv_heads + k, g * tree:(g + 1) * tree, :])
            return jnp.concatenate(pieces, axis=1)

        half = tokens // 2
        per_half = requests // 2
        copies = []

        def head_copy(s, start, rows):
            copy = pltpu.make_async_remote_copy(
                src_ref=product.at[pl.ds(start, rows)], dst_ref=head_stages[s],
                send_sem=head_send.at[s], recv_sem=head_recv.at[s],
                device_id={head_axis: head_plan[s][1]}, device_id_type=pl.DeviceIdType.MESH,
            )
            copy.start()
            copies.append(copy)
            return copy

        first_bit = head_plan[0][0]
        for turn in range(2):
            side = (1 - first_bit) if turn == 0 else first_bit
            rows = jnp.concatenate([rows_of(side * per_half + q) for q in range(per_half)], axis=0)
            product[pl.ds(side * half, half), :] = jnp.dot(
                rows, w_ref[...], preferred_element_type=jnp.float32)
            if turn == 0:
                copy = head_copy(0, side * half, half)
        base, size = first_bit * half, half
        for s in range(len(head_stages)):
            if s > 0:
                size = size // 2
                copy = head_copy(s, base + (1 - head_plan[s][0]) * size, size)
                base = base + head_plan[s][0] * size
            copy.wait_recv()
            total = product[pl.ds(base, size), :] + head_stages[s][...]
            if s + 1 < len(head_stages):
                product[pl.ds(base, size), :] = total
            else:
                out_ref[...] = total.astype(out_ref.dtype)
        for copy in copies:
            copy.wait_send()
    for copy in waits:
        copy.wait_send()


def body(queries, new_keys, new_values, cache_keys, cache_values, parents, kv_lengths, out_weight):
    requests, tree, heads, head_size = queries.shape
    kv_heads = new_keys.shape[2]
    group = heads // kv_heads
    block_size = cache_keys.shape[1]
    n = lax.axis_size("seq")
    stages = n.bit_length() - 1
    pairs = requests * kv_heads
    split = max(1, n // pairs)
    columns = group * tree
    deep = head_size * pairs // n
    lanes = min(128, columns)
    streams = columns // lanes
    me = lax.axis_index("seq")
    score_scale = math.log2(math.e) / math.sqrt(head_size)

    def by_head(array):
        return array.transpose(0, 2, 1, 3).reshape(pairs, array.shape[1], head_size)

    q = queries.reshape(requests, tree, kv_heads, group, head_size).transpose(0, 2, 3, 1, 4)
    q = q.reshape(pairs, columns, head_size)
    parent_rows = jnp.broadcast_to(jnp.tile(parents, (1, group))[:, None, :], (requests, 8, columns))

    def pair_block(rows):
        return pl.BlockSpec((None, rows, head_size), lambda p, *_: (p, 0, 0))

    o, ml = pl.pallas_call(
        functools.partial(attend_kernel, kv_heads, split, stages, score_scale),
        grid_spec=pltpu.PrefetchScalarGridSpec(
            num_scalar_prefetch=2,
            grid=(pairs,),
            in_specs=[
                pair_block(columns), pair_block(block_size), pair_block(block_size),
                pair_block(tree), pair_block(tree),
                pl.BlockSpec((None, 8, columns), lambda p, *_: (p // kv_heads, 0, 0)),
            ],
            out_specs=[
                pl.BlockSpec((streams, None, head_size, lanes), lambda p, *_: (0, p, 0, 0)),
                pl.BlockSpec((streams, None, 2, lanes), lambda p, *_: (0, p, 0, 0)),
            ],
        ),
        out_shape=[
            jax.ShapeDtypeStruct((streams, pairs, head_size, lanes), jnp.bfloat16),
            jax.ShapeDtypeStruct((streams, pairs, 2, lanes), jnp.float32),
        ],
        compiler_params=pltpu.CompilerParams(vmem_limit_bytes=48 * 1024 * 1024),
    )(kv_lengths, me[None].astype(jnp.int32), q, by_head(cache_keys), by_head(cache_values),
      by_head(new_keys), by_head(new_values), parent_rows)

    fused = (requests, tree) if n == pairs and lanes == head_size else None
    o = o.reshape(streams, n, deep, lanes)
    halves = [n >> (s + 1) for s in range(stages)]
    masks = [1 << s for s in range(stages)]
    if stages > 3:
        masks[3] = 12
    order = list(range(stages))
    turned = order[:1] + order[2:] + order[1:2]
    orders = [turned if t % 2 else order for t in range(streams)]

    def buffers(rows, kind):
        return [pltpu.VMEM((streams, h, rows, lanes), kind) for h in halves]

    ml_bufs = [pltpu.VMEM((streams, max(1, h // split), 2, lanes), jnp.float32) for h in halves]
    scratch = (buffers(deep, jnp.float32) + buffers(deep, jnp.bfloat16) + buffers(deep, jnp.bfloat16)
               + ml_bufs + ml_bufs + [pltpu.SemaphoreType.DMA((3 * stages * streams,))] * 2)
    vmem = pl.BlockSpec(memory_space=pltpu.VMEM)
    params = pltpu.CompilerParams(collective_id=0, has_side_effects=True, vmem_limit_bytes=48 * 1024 * 1024)
    if fused:
        tokens, width = requests * tree, out_weight.shape[1]
        count = lax.axis_size("head")
        head_bufs = [pltpu.VMEM((tokens >> (s + 1), width), jnp.float32) for s in range(count.bit_length() - 1)]
        return pl.pallas_call(
            functools.partial(merge_kernel, n, stages, split, orders, masks, "head", fused),
            out_shape=jax.ShapeDtypeStruct((tokens // count, width), jnp.bfloat16),
            in_specs=[vmem, vmem, vmem],
            out_specs=vmem,
            scratch_shapes=scratch
            + [pltpu.VMEM((streams, n, lanes, head_size), jnp.bfloat16), pltpu.VMEM((tokens, width), jnp.float32)]
            + head_bufs + [pltpu.SemaphoreType.DMA((len(head_bufs),))] * 2,
            compiler_params=params,
        )(o, ml, out_weight)
    gathered = pl.pallas_call(
        functools.partial(merge_kernel, n, stages, split, orders, masks, "head", fused),
        out_shape=jax.ShapeDtypeStruct((streams, n, deep, lanes), jnp.bfloat16),
        in_specs=[vmem, vmem],
        out_specs=vmem,
        scratch_shapes=scratch,
        compiler_params=params,
    )(o, ml)
    attended = gathered.reshape(streams, requests, kv_heads, head_size, lanes).transpose(1, 2, 0, 4, 3)
    attended = attended.reshape(requests, kv_heads, group, tree, head_size).transpose(0, 3, 1, 2, 4)
    attended = attended.reshape(requests * tree, heads * head_size)
    mixed = lax.psum_scatter(
        jnp.dot(attended, out_weight, preferred_element_type=jnp.float32),
        "head",
        scatter_dimension=0,
        tiled=True,
    )
    return mixed.astype(jnp.bfloat16)


def solution(mesh):
    placed = (
        P(None, None, "head", None),
        P(None, None, "head", None),
        P(None, None, "head", None),
        P(None, "seq", "head", None),
        P(None, "seq", "head", None),
        P(),
        P(),
        P("head", "seq"),
    )
    return jax.shard_map(
        body, mesh=mesh, in_specs=placed, out_specs=P("head", "seq"), check_vma=False
    )
```

```python
import functools
import math

import jax
import jax.numpy as jnp
from jax import lax
from jax.experimental import pallas as pl
from jax.experimental.pallas import tpu as pltpu
from jax.sharding import PartitionSpec as P

lowest = -1e30
NT = (((1,), (1,)), ((), ()))
TN = (((0,), (0,)), ((), ()))


def bit_reversed(index, stages):
    result = index * 0
    for stage in range(stages):
        result = result * 2 + (index // (1 << stage)) % 2
    return result


def attend_kernel(kv_heads, split, stages, score_scale, lengths_ref, place_ref, q_ref, k_ref, v_ref,
                  tk_ref, tv_ref, parents_ref, o_ref, ml_ref, *scratch):
    step = pl.program_id(0)
    block_size = k_ref.shape[0]
    head = step % kv_heads
    columns = q_ref.shape[0]
    tile = columns
    streams, _, lanes = o_ref.shape
    request = step // kv_heads
    me = place_ref[0]
    valid = lengths_ref[request] - me * block_size
    if scratch:
        keys_ref, values_ref, tree_keys_ref, tree_values_ref = scratch

        @pl.when((head == 0) & (valid > 0))
        def _():
            keys_ref[...] = jnp.swapaxes(k_ref[...], 0, 1)
            values_ref[...] = jnp.swapaxes(v_ref[...], 0, 1)

    def keys_of(ref, split_ref):
        return split_ref[head] if scratch else ref[...]

    if not scratch:
        keys_ref = values_ref = tree_keys_ref = tree_values_ref = None

    def write(masked):
        for start in range(0, columns, tile):
            here = pl.ds(start, tile)
            s = lax.dot_general(keys_of(k_ref, keys_ref), q_ref[here, :], NT, preferred_element_type=jnp.float32)
            if masked:
                rows = lax.broadcasted_iota(jnp.int32, s.shape, 0)
                s = jnp.where(rows < valid, s, lowest)
            m = jnp.max(s, axis=0, keepdims=True) * score_scale
            w = jnp.exp2(s * score_scale - m)
            tot = jnp.sum(w, axis=0, keepdims=True)
            acc = lax.dot_general(
                keys_of(v_ref, values_ref), w.astype(jnp.bfloat16), TN, preferred_element_type=jnp.float32
            ).astype(o_ref.dtype)
            for inner in range(0, tile, lanes):
                t = (start + inner) // lanes
                ml_ref[t, 0:1, :] = m[:, inner:inner + lanes]
                ml_ref[t, 1:2, :] = tot[:, inner:inner + lanes]
                o_ref[t] = acc[:, inner:inner + lanes]

    @pl.when(valid >= block_size)
    def _():
        write(False)

    @pl.when((valid > 0) & (valid < block_size))
    def _():
        write(True)

    @pl.when(valid <= 0)
    def _():
        o_ref[...] = jnp.zeros_like(o_ref)
        ml_ref[:, 0:1, :] = jnp.full((streams, 1, lanes), lowest, jnp.float32)
        ml_ref[:, 1:2, :] = jnp.zeros((streams, 1, lanes), jnp.float32)

    own = bit_reversed(me, stages)

    @pl.when((own // split == step) & (own % split == 0))
    def _():
        tree = tk_ref.shape[0]
        if scratch:
            tree_keys_ref[...] = jnp.swapaxes(tk_ref[...], 0, 1)
            tree_values_ref[...] = jnp.swapaxes(tv_ref[...], 0, 1)

        def reach(parent_row):
            width = parent_row.shape[1]
            key = lax.broadcasted_iota(jnp.int32, (tree, width), 0)
            token = lax.broadcasted_iota(jnp.int32, (tree, width), 1) % tree
            hit = (parent_row == key) | (token == key)
            return jnp.where(hit, 1.0, 0.0)

        wide = reach(jnp.concatenate([parents_ref[pl.ds(request, 1), :]] * (columns // tree), axis=1))
        square = wide[:, :tree]
        for _ in range(max(1, (tree - 1).bit_length())):
            left = square.astype(jnp.bfloat16)
            wide = jnp.minimum(jnp.dot(left, wide.astype(jnp.bfloat16), preferred_element_type=jnp.float32), 1.0)
            square = wide[:, :tree]
        s = lax.dot_general(keys_of(tk_ref, tree_keys_ref), q_ref[...], NT, preferred_element_type=jnp.float32)
        allowed = wide > 0.5
        s = jnp.where(allowed, s * score_scale, lowest)
        m = jnp.max(s, axis=0, keepdims=True)
        w = jnp.where(allowed, jnp.exp2(s - m), 0.0)
        tot = jnp.sum(w, axis=0, keepdims=True)
        acc = lax.dot_general(keys_of(tv_ref, tree_values_ref), w.astype(jnp.bfloat16), TN, preferred_element_type=jnp.float32)
        for t in range(streams):
            here = slice(t * lanes, (t + 1) * lanes)
            m_old = ml_ref[t, 0:1, :]
            m_new = jnp.maximum(m_old, m[:, here])
            f_old, f_tree = jnp.exp2(m_old - m_new), jnp.exp2(m[:, here] - m_new)
            ml_ref[t, 1:2, :] = ml_ref[t, 1:2, :] * f_old + tot[:, here] * f_tree
            ml_ref[t, 0:1, :] = m_new
            o_ref[t] = (o_ref[t].astype(jnp.float32) * f_old + acc[:, here] * f_tree).astype(o_ref.dtype)


def merge_kernel(n, stages, split, orders, masks, head_axis, fused, o_ref, ml_ref, *refs):
    streams = len(orders)
    if fused:
        w_ref, out_ref, *scratch = refs
    else:
        g_ref, *scratch = refs
    scratch = list(scratch)

    def take(count):
        taken = scratch[:count]
        del scratch[:count]
        return taken

    o_sum, o_out, o_in, ml_out, ml_in = (take(stages) for _ in range(5))
    (send, recv) = take(2)
    me = lax.axis_index("seq")

    def bit(position):
        return (me // (1 << position)) % 2

    partners, bits = [], []
    for position in range(stages):
        move = 0
        for q in range(stages):
            if (masks[position] >> q) & 1:
                move = move + (1 - 2 * bit(q)) * (1 << q)
        partners.append(me + move)
        value = bit(position)
        for other in range(position + 1, stages):
            if (masks[other] >> position) & 1:
                value = (value + bit(other)) % 2
        bits.append(value)

    head_stages = []
    if fused:
        (attended, product) = take(2)
        head_count = lax.axis_size(head_axis)
        head_stages = take(head_count.bit_length() - 1)
        (head_send, head_recv) = take(2)
        head = lax.axis_index(head_axis)

    barrier = pltpu.get_barrier_semaphore()
    for partner in partners:
        pl.semaphore_signal(barrier, inc=1, device_id={"seq": partner}, device_id_type=pl.DeviceIdType.MESH)
    head_plan = []
    for s in range(len(head_stages)):
        stride = head_count >> (s + 1)
        head_bit = (head // stride) % 2
        partner = head + (1 - 2 * head_bit) * stride
        head_plan.append((head_bit, partner))
        pl.semaphore_signal(barrier, inc=1, device_id={head_axis: partner}, device_id_type=pl.DeviceIdType.MESH)
    pl.semaphore_wait(barrier, stages + len(head_stages))

    def remote(src, dst, slot, position):
        return pltpu.make_async_remote_copy(
            src_ref=src, dst_ref=dst, send_sem=send.at[slot], recv_sem=recv.at[slot],
            device_id={"seq": partners[position]}, device_id_type=pl.DeviceIdType.MESH,
        )

    waits = []
    flying = {}

    def begin(t, s):
        position = orders[t][s]
        half = n >> (s + 1)
        pairs = max(1, half // split)
        away = (1 - bits[position]) * half
        pair_away = (1 - bits[position]) * pairs if half >= split else 0
        o_src = o_ref if s == 0 else o_out[s - 1]
        ml_src = ml_ref if s == 0 else ml_out[s - 1]
        slot = (t * stages + s) * 3
        small = remote(ml_src.at[t, pl.ds(pair_away, pairs)], ml_in[s].at[t], slot, position)
        large = remote(o_src.at[t, pl.ds(away, half)], o_in[s].at[t], slot + 1, position)
        small.start()
        large.start()
        waits.extend([small, large])
        flying[t] = (small, large)

    def finish(t, s):
        position = orders[t][s]
        half = n >> (s + 1)
        pairs = max(1, half // split)
        keep = bits[position] * half
        pair_keep = bits[position] * pairs if half >= split else 0
        per_pair = half // pairs
        small, large = flying[t]
        small.wait_recv()
        large.wait_recv()
        ml_src = ml_ref if s == 0 else ml_out[s - 1]
        o_src = o_ref if s == 0 else o_sum[s - 1]

        def one_pair(p, carry):
            m_a, m_b = ml_src[t, pair_keep + p, 0:1, :], ml_in[s][t, p, 0:1, :]
            l_a, l_b = ml_src[t, pair_keep + p, 1:2, :], ml_in[s][t, p, 1:2, :]
            m = jnp.maximum(m_a, m_b)
            f_a, f_b = jnp.exp2(m_a - m), jnp.exp2(m_b - m)
            ml_out[s][t, p, 0:1, :] = m
            ml_out[s][t, p, 1:2, :] = l_a * f_a + l_b * f_b
            for c in range(per_pair):
                at = p * per_pair + c
                mine = o_src[t, keep + at].astype(jnp.float32)
                theirs = o_in[s][t, at].astype(jnp.float32)
                total = mine * f_a + theirs * f_b
                o_sum[s][t, at] = total
                o_out[s][t, at] = total.astype(jnp.bfloat16)
            return carry

        lax.fori_loop(0, pairs, one_pair, 0)

    for t in range(streams):
        begin(t, 0)
    lows = [0] * streams
    gathered = attended if fused else g_ref

    def gather(t, s):
        size = n >> (s + 1)
        start = (lows[t] // size) * size
        block = gathered.at[t, pl.ds(start, size)]
        copy = remote(block, block, (t * stages + s) * 3 + 2, orders[t][s])
        copy.start()
        waits.append(copy)
        flying[t] = copy

    for s in range(stages):
        for t in range(streams):
            finish(t, s)
            if s + 1 < stages:
                begin(t, s + 1)
            else:
                low = 0
                for position in orders[t]:
                    low = low * 2 + bits[position]
                lows[t] = low
                share = o_sum[s][t, 0] / ml_out[s][t, 0, 1:2, :]
                if fused:
                    share = share.T
                gathered[t, low] = share.astype(jnp.bfloat16)
                gather(t, s)
    for s in reversed(range(stages)):
        for t in range(streams):
            flying[t].wait_recv()
            if s > 0:
                gather(t, s - 1)

    if fused:
        tokens, width = product.shape
        requests, tree = fused
        kv_heads = n // requests
        parts = attended.shape[2] // tree
        groups = streams * parts
        head_size = attended.shape[3]

        def rows_of(request):
            pieces = []
            for k in range(kv_heads):
                for t in range(streams):
                    for g in range(parts):
                        pieces.append(attended[t, request * kv_heads + k, g * tree:(g + 1) * tree, :])
            return jnp.concatenate(pieces, axis=1)

        half = tokens // 2
        per_half = requests // 2
        copies = []

        def head_copy(s, start, rows):
            copy = pltpu.make_async_remote_copy(
                src_ref=product.at[pl.ds(start, rows)], dst_ref=head_stages[s],
                send_sem=head_send.at[s], recv_sem=head_recv.at[s],
                device_id={head_axis: head_plan[s][1]}, device_id_type=pl.DeviceIdType.MESH,
            )
            copy.start()
            copies.append(copy)
            return copy

        first_bit = head_plan[0][0]
        for turn in range(2):
            side = (1 - first_bit) if turn == 0 else first_bit
            rows = jnp.concatenate([rows_of(side * per_half + q) for q in range(per_half)], axis=0)
            product[pl.ds(side * half, half), :] = jnp.dot(
                rows, w_ref[...], preferred_element_type=jnp.float32)
            if turn == 0:
                copy = head_copy(0, side * half, half)
        base, size = first_bit * half, half
        for s in range(len(head_stages)):
            if s > 0:
                size = size // 2
                copy = head_copy(s, base + (1 - head_plan[s][0]) * size, size)
                base = base + head_plan[s][0] * size
            copy.wait_recv()
            total = product[pl.ds(base, size), :] + head_stages[s][...]
            if s + 1 < len(head_stages):
                product[pl.ds(base, size), :] = total
            else:
                out_ref[...] = total.astype(out_ref.dtype)
        for copy in copies:
            copy.wait_send()
    for copy in waits:
        copy.wait_send()


def body(queries, new_keys, new_values, cache_keys, cache_values, parents, kv_lengths, out_weight):
    requests, tree, heads, head_size = queries.shape
    kv_heads = new_keys.shape[2]
    group = heads // kv_heads
    block_size = cache_keys.shape[1]
    n = lax.axis_size("seq")
    stages = n.bit_length() - 1
    pairs = requests * kv_heads
    split = max(1, n // pairs)
    columns = group * tree
    deep = head_size * pairs // n
    lanes = min(128, columns)
    streams = columns // lanes
    me = lax.axis_index("seq")
    score_scale = math.log2(math.e) / math.sqrt(head_size)

    def by_head(array):
        return array.transpose(0, 2, 1, 3).reshape(pairs, array.shape[1], head_size)

    q = queries.reshape(requests, tree, kv_heads, group, head_size).transpose(0, 2, 3, 1, 4)
    q = q.reshape(pairs, columns, head_size)

    inside = kv_heads % 4 == 0
    if not inside:
        cache_keys, cache_values, new_keys, new_values = map(by_head, (cache_keys, cache_values, new_keys, new_values))
    split_scratch = [pltpu.VMEM((kv_heads, rows, head_size), jnp.bfloat16)
                     for rows in (block_size, block_size, tree, tree) if inside]

    def key_block(rows):
        if inside:
            return pl.BlockSpec((None, rows, kv_heads, head_size), lambda p, *_: (p // kv_heads, 0, 0, 0))
        return pair_block(rows)

    def pair_block(rows):
        return pl.BlockSpec((None, rows, head_size), lambda p, *_: (p, 0, 0))

    o, ml = pl.pallas_call(
        functools.partial(attend_kernel, kv_heads, split, stages, score_scale),
        grid_spec=pltpu.PrefetchScalarGridSpec(
            num_scalar_prefetch=2,
            grid=(pairs,),
            in_specs=[
                pair_block(columns), key_block(block_size), key_block(block_size),
                key_block(tree), key_block(tree),
                pl.BlockSpec(parents.shape, lambda p, *_: (0, 0)),
            ],
            out_specs=[
                pl.BlockSpec((streams, None, head_size, lanes), lambda p, *_: (0, p, 0, 0)),
                pl.BlockSpec((streams, None, 2, lanes), lambda p, *_: (0, p, 0, 0)),
            ],
            scratch_shapes=split_scratch,
        ),
        out_shape=[
            jax.ShapeDtypeStruct((streams, pairs, head_size, lanes), jnp.bfloat16),
            jax.ShapeDtypeStruct((streams, pairs, 2, lanes), jnp.float32),
        ],
        compiler_params=pltpu.CompilerParams(vmem_limit_bytes=48 * 1024 * 1024),
    )(kv_lengths, me[None].astype(jnp.int32), q, cache_keys, cache_values, new_keys, new_values, parents)

    fused = (requests, tree) if n == pairs and lanes == head_size else None
    o = o.reshape(streams, n, deep, lanes)
    halves = [n >> (s + 1) for s in range(stages)]
    masks = [1 << s for s in range(stages)]
    if stages > 3:
        masks[3] = 12
    order = list(range(stages))
    turned = order[:1] + order[2:] + order[1:2]
    orders = [turned if t % 2 else order for t in range(streams)]

    def buffers(rows, kind):
        return [pltpu.VMEM((streams, h, rows, lanes), kind) for h in halves]

    ml_bufs = [pltpu.VMEM((streams, max(1, h // split), 2, lanes), jnp.float32) for h in halves]
    scratch = (buffers(deep, jnp.float32) + buffers(deep, jnp.bfloat16) + buffers(deep, jnp.bfloat16)
               + ml_bufs + ml_bufs + [pltpu.SemaphoreType.DMA((3 * stages * streams,))] * 2)
    vmem = pl.BlockSpec(memory_space=pltpu.VMEM)
    params = pltpu.CompilerParams(collective_id=0, has_side_effects=True, vmem_limit_bytes=48 * 1024 * 1024)
    if fused:
        tokens, width = requests * tree, out_weight.shape[1]
        count = lax.axis_size("head")
        head_bufs = [pltpu.VMEM((tokens >> (s + 1), width), jnp.float32) for s in range(count.bit_length() - 1)]
        return pl.pallas_call(
            functools.partial(merge_kernel, n, stages, split, orders, masks, "head", fused),
            out_shape=jax.ShapeDtypeStruct((tokens // count, width), jnp.bfloat16),
            in_specs=[vmem, vmem, vmem],
            out_specs=vmem,
            scratch_shapes=scratch
            + [pltpu.VMEM((streams, n, lanes, head_size), jnp.bfloat16), pltpu.VMEM((tokens, width), jnp.float32)]
            + head_bufs + [pltpu.SemaphoreType.DMA((len(head_bufs),))] * 2,
            compiler_params=params,
        )(o, ml, out_weight)
    gathered = pl.pallas_call(
        functools.partial(merge_kernel, n, stages, split, orders, masks, "head", fused),
        out_shape=jax.ShapeDtypeStruct((streams, n, deep, lanes), jnp.bfloat16),
        in_specs=[vmem, vmem],
        out_specs=vmem,
        scratch_shapes=scratch,
        compiler_params=params,
    )(o, ml)
    attended = gathered.reshape(streams, requests, kv_heads, head_size, lanes).transpose(1, 2, 0, 4, 3)
    attended = attended.reshape(requests, kv_heads, group, tree, head_size).transpose(0, 3, 1, 2, 4)
    attended = attended.reshape(requests * tree, heads * head_size)
    mixed = lax.psum_scatter(
        jnp.dot(attended, out_weight, preferred_element_type=jnp.float32),
        "head",
        scatter_dimension=0,
        tiled=True,
    )
    return mixed.astype(jnp.bfloat16)


def solution(mesh):
    placed = (
        P(None, None, "head", None),
        P(None, None, "head", None),
        P(None, None, "head", None),
        P(None, "seq", "head", None),
        P(None, "seq", "head", None),
        P(),
        P(),
        P("head", "seq"),
    )
    return jax.shard_map(
        body, mesh=mesh, in_specs=placed, out_specs=P("head", "seq"), check_vma=False
    )
```

```python
import functools
import math

import jax
import jax.numpy as jnp
from jax import lax
from jax.experimental import pallas as pl
from jax.experimental.pallas import tpu as pltpu
from jax.sharding import PartitionSpec as P

lowest = -1e30
NT = (((1,), (1,)), ((), ()))
TN = (((0,), (0,)), ((), ()))


def bit_reversed(index, stages):
    result = index * 0
    for stage in range(stages):
        result = result * 2 + (index // (1 << stage)) % 2
    return result


def split_heads(source, target):
    rows, kv_heads, head_size = source.shape
    flat = source[...].reshape(rows, kv_heads * head_size)
    for h in range(kv_heads):
        target[h] = flat[:, h * head_size:(h + 1) * head_size]


def attend_kernel(kv_heads, split, stages, score_scale, lengths_ref, place_ref, q_ref, k_ref, v_ref,
                  tk_ref, tv_ref, parents_ref, o_ref, ml_ref, *scratch):
    step = pl.program_id(0)
    block_size = k_ref.shape[0]
    head = step % kv_heads
    streams, _, lanes = o_ref.shape
    columns = streams * lanes
    request = step // kv_heads
    me = place_ref[0]
    valid = lengths_ref[request] - me * block_size
    if scratch:
        keys_ref, values_ref, tree_keys_ref, tree_values_ref, queries_ref = scratch

        @pl.when((head == 0) & (valid > 0))
        def _():
            split_heads(k_ref, keys_ref)
            split_heads(v_ref, values_ref)

        @pl.when(head == 0)
        def _():
            tokens, heads, head_size = q_ref.shape
            flat = q_ref[...].reshape(tokens, heads * head_size)
            group = heads // kv_heads
            for h in range(heads):
                queries_ref[h // group, (h % group) * tokens:(h % group + 1) * tokens, :] = (
                    flat[:, h * head_size:(h + 1) * head_size])

    def keys_of(ref, split_ref):
        return split_ref[head] if scratch else ref[...]

    if not scratch:
        keys_ref = values_ref = tree_keys_ref = tree_values_ref = queries_ref = None

    def write(masked):
        for start in (0,):
            tile = columns
            s = lax.dot_general(keys_of(k_ref, keys_ref), keys_of(q_ref, queries_ref), NT, preferred_element_type=jnp.float32)
            if masked:
                rows = lax.broadcasted_iota(jnp.int32, s.shape, 0)
                s = jnp.where(rows < valid, s, lowest)
            m = jnp.max(s, axis=0, keepdims=True) * score_scale
            w = jnp.exp2(s * score_scale - m)
            tot = jnp.sum(w, axis=0, keepdims=True)
            acc = lax.dot_general(
                keys_of(v_ref, values_ref), w.astype(jnp.bfloat16), TN, preferred_element_type=jnp.float32
            ).astype(o_ref.dtype)
            for inner in range(0, tile, lanes):
                t = (start + inner) // lanes
                ml_ref[t, 0:1, :] = m[:, inner:inner + lanes]
                ml_ref[t, 1:2, :] = tot[:, inner:inner + lanes]
                o_ref[t] = acc[:, inner:inner + lanes]

    @pl.when(valid >= block_size)
    def _():
        write(False)

    @pl.when((valid > 0) & (valid < block_size))
    def _():
        write(True)

    @pl.when(valid <= 0)
    def _():
        o_ref[...] = jnp.zeros_like(o_ref)
        ml_ref[:, 0:1, :] = jnp.full((streams, 1, lanes), lowest, jnp.float32)
        ml_ref[:, 1:2, :] = jnp.zeros((streams, 1, lanes), jnp.float32)

    own = bit_reversed(me, stages)

    @pl.when((own // split == step) & (own % split == 0))
    def _():
        tree = tk_ref.shape[0]
        if scratch:
            tree_keys_ref[...] = jnp.swapaxes(tk_ref[...], 0, 1)
            tree_values_ref[...] = jnp.swapaxes(tv_ref[...], 0, 1)

        def reach(parent_row):
            width = parent_row.shape[1]
            key = lax.broadcasted_iota(jnp.int32, (tree, width), 0)
            token = lax.broadcasted_iota(jnp.int32, (tree, width), 1) % tree
            hit = (parent_row == key) | (token == key)
            return jnp.where(hit, 1.0, 0.0)

        wide = reach(jnp.concatenate([parents_ref[pl.ds(request, 1), :]] * (columns // tree), axis=1))
        square = wide[:, :tree]
        for _ in range(max(1, (tree - 1).bit_length())):
            left = square.astype(jnp.bfloat16)
            wide = jnp.minimum(jnp.dot(left, wide.astype(jnp.bfloat16), preferred_element_type=jnp.float32), 1.0)
            square = wide[:, :tree]
        s = lax.dot_general(keys_of(tk_ref, tree_keys_ref), keys_of(q_ref, queries_ref), NT, preferred_element_type=jnp.float32)
        allowed = wide > 0.5
        s = jnp.where(allowed, s * score_scale, lowest)
        m = jnp.max(s, axis=0, keepdims=True)
        w = jnp.where(allowed, jnp.exp2(s - m), 0.0)
        tot = jnp.sum(w, axis=0, keepdims=True)
        acc = lax.dot_general(keys_of(tv_ref, tree_values_ref), w.astype(jnp.bfloat16), TN, preferred_element_type=jnp.float32)
        for t in range(streams):
            here = slice(t * lanes, (t + 1) * lanes)
            m_old = ml_ref[t, 0:1, :]
            m_new = jnp.maximum(m_old, m[:, here])
            f_old, f_tree = jnp.exp2(m_old - m_new), jnp.exp2(m[:, here] - m_new)
            ml_ref[t, 1:2, :] = ml_ref[t, 1:2, :] * f_old + tot[:, here] * f_tree
            ml_ref[t, 0:1, :] = m_new
            o_ref[t] = (o_ref[t].astype(jnp.float32) * f_old + acc[:, here] * f_tree).astype(o_ref.dtype)


def merge_kernel(n, stages, split, orders, masks, head_axis, fused, o_ref, ml_ref, *refs):
    streams = len(orders)
    if fused:
        w_ref, out_ref, *scratch = refs
    else:
        g_ref, *scratch = refs
    scratch = list(scratch)

    def take(count):
        taken = scratch[:count]
        del scratch[:count]
        return taken

    o_sum, o_out, o_in, ml_out, ml_in = (take(stages) for _ in range(5))
    (send, recv) = take(2)
    me = lax.axis_index("seq")

    def bit(position):
        return (me // (1 << position)) % 2

    partners, bits = [], []
    for position in range(stages):
        move = 0
        for q in range(stages):
            if (masks[position] >> q) & 1:
                move = move + (1 - 2 * bit(q)) * (1 << q)
        partners.append(me + move)
        value = bit(position)
        for other in range(position + 1, stages):
            if (masks[other] >> position) & 1:
                value = (value + bit(other)) % 2
        bits.append(value)

    head_stages = []
    if fused:
        (attended, product) = take(2)
        head_count = lax.axis_size(head_axis)
        head_stages = take(head_count.bit_length() - 1)
        (head_send, head_recv) = take(2)
        head = lax.axis_index(head_axis)

    barrier = pltpu.get_barrier_semaphore()
    for partner in partners:
        pl.semaphore_signal(barrier, inc=1, device_id={"seq": partner}, device_id_type=pl.DeviceIdType.MESH)
    head_plan = []
    for s in range(len(head_stages)):
        stride = head_count >> (s + 1)
        head_bit = (head // stride) % 2
        partner = head + (1 - 2 * head_bit) * stride
        head_plan.append((head_bit, partner))
        pl.semaphore_signal(barrier, inc=1, device_id={head_axis: partner}, device_id_type=pl.DeviceIdType.MESH)
    pl.semaphore_wait(barrier, stages + len(head_stages))

    def remote(src, dst, slot, position):
        return pltpu.make_async_remote_copy(
            src_ref=src, dst_ref=dst, send_sem=send.at[slot], recv_sem=recv.at[slot],
            device_id={"seq": partners[position]}, device_id_type=pl.DeviceIdType.MESH,
        )

    waits = []
    flying = {}

    def begin(t, s):
        position = orders[t][s]
        half = n >> (s + 1)
        pairs = max(1, half // split)
        away = (1 - bits[position]) * half
        pair_away = (1 - bits[position]) * pairs if half >= split else 0
        o_src = o_ref if s == 0 else o_out[s - 1]
        ml_src = ml_ref if s == 0 else ml_out[s - 1]
        slot = (t * stages + s) * 3
        small = remote(ml_src.at[t, pl.ds(pair_away, pairs)], ml_in[s].at[t], slot, position)
        large = remote(o_src.at[t, pl.ds(away, half)], o_in[s].at[t], slot + 1, position)
        small.start()
        large.start()
        waits.extend([small, large])
        flying[t] = (small, large)

    def finish(t, s):
        position = orders[t][s]
        half = n >> (s + 1)
        pairs = max(1, half // split)
        keep = bits[position] * half
        pair_keep = bits[position] * pairs if half >= split else 0
        per_pair = half // pairs
        small, large = flying[t]
        small.wait_recv()
        large.wait_recv()
        ml_src = ml_ref if s == 0 else ml_out[s - 1]
        o_src = o_ref if s == 0 else o_sum[s - 1]

        def one_pair(p, carry):
            m_a, m_b = ml_src[t, pair_keep + p, 0:1, :], ml_in[s][t, p, 0:1, :]
            l_a, l_b = ml_src[t, pair_keep + p, 1:2, :], ml_in[s][t, p, 1:2, :]
            m = jnp.maximum(m_a, m_b)
            f_a, f_b = jnp.exp2(m_a - m), jnp.exp2(m_b - m)
            ml_out[s][t, p, 0:1, :] = m
            ml_out[s][t, p, 1:2, :] = l_a * f_a + l_b * f_b
            for c in range(per_pair):
                at = p * per_pair + c
                mine = o_src[t, keep + at].astype(jnp.float32)
                theirs = o_in[s][t, at].astype(jnp.float32)
                total = mine * f_a + theirs * f_b
                o_sum[s][t, at] = total
                o_out[s][t, at] = total.astype(jnp.bfloat16)
            return carry

        lax.fori_loop(0, pairs, one_pair, 0)

    for t in range(streams):
        begin(t, 0)
    lows = [0] * streams
    gathered = attended if fused else g_ref

    def gather(t, s):
        size = n >> (s + 1)
        start = (lows[t] // size) * size
        block = gathered.at[t, pl.ds(start, size)]
        copy = remote(block, block, (t * stages + s) * 3 + 2, orders[t][s])
        copy.start()
        waits.append(copy)
        flying[t] = copy

    for s in range(stages):
        for t in range(streams):
            finish(t, s)
            if s + 1 < stages:
                begin(t, s + 1)
            else:
                low = 0
                for position in orders[t]:
                    low = low * 2 + bits[position]
                lows[t] = low
                share = o_sum[s][t, 0] / ml_out[s][t, 0, 1:2, :]
                if fused:
                    share = share.T
                gathered[t, low] = share.astype(jnp.bfloat16)
                gather(t, s)
    for s in reversed(range(stages)):
        for t in range(streams):
            flying[t].wait_recv()
            if s > 0:
                gather(t, s - 1)

    if fused:
        tokens, width = product.shape
        requests, tree = fused
        kv_heads = n // requests
        parts = attended.shape[2] // tree
        groups = streams * parts
        head_size = attended.shape[3]

        def rows_of(request):
            pieces = []
            for k in range(kv_heads):
                for t in range(streams):
                    for g in range(parts):
                        pieces.append(attended[t, request * kv_heads + k, g * tree:(g + 1) * tree, :])
            return jnp.concatenate(pieces, axis=1)

        half = tokens // 2
        per_half = requests // 2
        copies = []

        def head_copy(s, start, rows):
            copy = pltpu.make_async_remote_copy(
                src_ref=product.at[pl.ds(start, rows)], dst_ref=head_stages[s],
                send_sem=head_send.at[s], recv_sem=head_recv.at[s],
                device_id={head_axis: head_plan[s][1]}, device_id_type=pl.DeviceIdType.MESH,
            )
            copy.start()
            copies.append(copy)
            return copy

        first_bit = head_plan[0][0]
        for turn in range(2):
            side = (1 - first_bit) if turn == 0 else first_bit
            rows = jnp.concatenate([rows_of(side * per_half + q) for q in range(per_half)], axis=0)
            product[pl.ds(side * half, half), :] = jnp.dot(
                rows, w_ref[...], preferred_element_type=jnp.float32)
            if turn == 0:
                copy = head_copy(0, side * half, half)
        base, size = first_bit * half, half
        for s in range(len(head_stages)):
            if s > 0:
                size = size // 2
                copy = head_copy(s, base + (1 - head_plan[s][0]) * size, size)
                base = base + head_plan[s][0] * size
            copy.wait_recv()
            total = product[pl.ds(base, size), :] + head_stages[s][...]
            if s + 1 < len(head_stages):
                product[pl.ds(base, size), :] = total
            else:
                out_ref[...] = total.astype(out_ref.dtype)
        for copy in copies:
            copy.wait_send()
    for copy in waits:
        copy.wait_send()


def body(queries, new_keys, new_values, cache_keys, cache_values, parents, kv_lengths, out_weight):
    requests, tree, heads, head_size = queries.shape
    kv_heads = new_keys.shape[2]
    group = heads // kv_heads
    block_size = cache_keys.shape[1]
    n = lax.axis_size("seq")
    stages = n.bit_length() - 1
    pairs = requests * kv_heads
    split = max(1, n // pairs)
    columns = group * tree
    deep = head_size * pairs // n
    lanes = min(128, columns)
    streams = columns // lanes
    me = lax.axis_index("seq")
    score_scale = math.log2(math.e) / math.sqrt(head_size)

    def by_head(array):
        return array.transpose(0, 2, 1, 3).reshape(pairs, array.shape[1], head_size)

    q = queries

    inside = kv_heads % 4 == 0
    if not inside:
        q = queries.reshape(requests, tree, kv_heads, group, head_size).transpose(0, 2, 3, 1, 4)
        q = q.reshape(pairs, columns, head_size)
        cache_keys, cache_values, new_keys, new_values = map(by_head, (cache_keys, cache_values, new_keys, new_values))
    split_scratch = [pltpu.VMEM((kv_heads, rows, head_size), jnp.bfloat16)
                     for rows in (block_size, block_size, tree, tree, columns) if inside]

    def key_block(rows):
        if inside:
            return pl.BlockSpec((None, rows, kv_heads, head_size), lambda p, *_: (p // kv_heads, 0, 0, 0))
        return pair_block(rows)

    def pair_block(rows):
        return pl.BlockSpec((None, rows, head_size), lambda p, *_: (p, 0, 0))

    query_block = pair_block(columns)
    if inside:
        query_block = pl.BlockSpec((None,) + queries.shape[1:], lambda p, *_: (p // kv_heads, 0, 0, 0))

    o, ml = pl.pallas_call(
        functools.partial(attend_kernel, kv_heads, split, stages, score_scale),
        grid_spec=pltpu.PrefetchScalarGridSpec(
            num_scalar_prefetch=2,
            grid=(pairs,),
            in_specs=[
                query_block, key_block(block_size), key_block(block_size),
                key_block(tree), key_block(tree),
                pl.BlockSpec(parents.shape, lambda p, *_: (0, 0)),
            ],
            out_specs=[
                pl.BlockSpec((streams, None, head_size, lanes), lambda p, *_: (0, p, 0, 0)),
                pl.BlockSpec((streams, None, 2, lanes), lambda p, *_: (0, p, 0, 0)),
            ],
            scratch_shapes=split_scratch,
        ),
        out_shape=[
            jax.ShapeDtypeStruct((streams, pairs, head_size, lanes), jnp.bfloat16),
            jax.ShapeDtypeStruct((streams, pairs, 2, lanes), jnp.float32),
        ],
        compiler_params=pltpu.CompilerParams(vmem_limit_bytes=48 * 1024 * 1024),
    )(kv_lengths, me[None].astype(jnp.int32), q, cache_keys, cache_values, new_keys, new_values, parents)

    fused = (requests, tree) if n == pairs and lanes == head_size else None
    o = o.reshape(streams, n, deep, lanes)
    halves = [n >> (s + 1) for s in range(stages)]
    masks = [1 << s for s in range(stages)]
    if stages > 3:
        masks[3] = 12
    order = list(range(stages))
    turned = order[:1] + order[2:] + order[1:2]
    orders = [turned if t % 2 else order for t in range(streams)]

    def buffers(rows, kind):
        return [pltpu.VMEM((streams, h, rows, lanes), kind) for h in halves]

    ml_bufs = [pltpu.VMEM((streams, max(1, h // split), 2, lanes), jnp.float32) for h in halves]
    scratch = (buffers(deep, jnp.float32) + buffers(deep, jnp.bfloat16) + buffers(deep, jnp.bfloat16)
               + ml_bufs + ml_bufs + [pltpu.SemaphoreType.DMA((3 * stages * streams,))] * 2)
    vmem = pl.BlockSpec(memory_space=pltpu.VMEM)
    params = pltpu.CompilerParams(collective_id=0, has_side_effects=True, vmem_limit_bytes=48 * 1024 * 1024)
    if fused:
        tokens, width = requests * tree, out_weight.shape[1]
        count = lax.axis_size("head")
        head_bufs = [pltpu.VMEM((tokens >> (s + 1), width), jnp.float32) for s in range(count.bit_length() - 1)]
        return pl.pallas_call(
            functools.partial(merge_kernel, n, stages, split, orders, masks, "head", fused),
            out_shape=jax.ShapeDtypeStruct((tokens // count, width), jnp.bfloat16),
            in_specs=[vmem, vmem, vmem],
            out_specs=vmem,
            scratch_shapes=scratch
            + [pltpu.VMEM((streams, n, lanes, head_size), jnp.bfloat16), pltpu.VMEM((tokens, width), jnp.float32)]
            + head_bufs + [pltpu.SemaphoreType.DMA((len(head_bufs),))] * 2,
            compiler_params=params,
        )(o, ml, out_weight)
    gathered = pl.pallas_call(
        functools.partial(merge_kernel, n, stages, split, orders, masks, "head", fused),
        out_shape=jax.ShapeDtypeStruct((streams, n, deep, lanes), jnp.bfloat16),
        in_specs=[vmem, vmem],
        out_specs=vmem,
        scratch_shapes=scratch,
        compiler_params=params,
    )(o, ml)
    attended = gathered.reshape(streams, requests, kv_heads, head_size, lanes).transpose(1, 2, 0, 4, 3)
    attended = attended.reshape(requests, kv_heads, group, tree, head_size).transpose(0, 3, 1, 2, 4)
    attended = attended.reshape(requests * tree, heads * head_size)
    mixed = lax.psum_scatter(
        jnp.dot(attended, out_weight, preferred_element_type=jnp.float32),
        "head",
        scatter_dimension=0,
        tiled=True,
    )
    return mixed.astype(jnp.bfloat16)


def solution(mesh):
    placed = (
        P(None, None, "head", None),
        P(None, None, "head", None),
        P(None, None, "head", None),
        P(None, "seq", "head", None),
        P(None, "seq", "head", None),
        P(),
        P(),
        P("head", "seq"),
    )
    return jax.shard_map(
        body, mesh=mesh, in_specs=placed, out_specs=P("head", "seq"), check_vma=False
    )
```
